32 devices in a mesh: replica: 2 (over core), shard: 16 (over z, y, x).
Axes of the slice: x: 2, y: 2, z: 4, core: 2. Of those that a mesh axis runs over, the one named last changes fastest.
Arguments:
- dense_input: bfloat16 [4096, 256], P(('replica', 'shard')), may hold values from -6 to 6
- bag_rows: int32 [4096, 2, 16], P(('replica', 'shard')), may hold values from 0 to 8191, as said below
- bag_lengths: int32 [4096, 2], P(('replica', 'shard')), may hold values from 1 to 16
- bag_weights: bfloat16 [4096, 2, 16], P(('replica', 'shard')), may hold values from 0.5 to 2
- labels: int32 [4096], P(('replica', 'shard')), may hold values 0 or 1
- embedding: float32 [8192, 2, 256], P('shard'), may hold values from -2 to 2
- first_moment: float32 [8192, 2, 256], P('shard'), may hold values from -6 to 6
- second_moment: float32 [8192, 2], P('shard'), may hold values from 0.5 to 8
- cross_weight: bfloat16 [768, 768], replicated, may hold values from -0.21875 to 0.21875
- hidden_weight: bfloat16 [768, 4096], replicated, may hold values from -0.21875 to 0.21875
- head_weight: bfloat16 [4096], replicated, may hold values from -0.09375 to 0.09375
Outputs:
- new_first: float32 [8192, 2, 256], P('shard')
- new_second: float32 [8192, 2], P('shard')
- row_step: float32 [8192, 2, 256], P('shard')
The draws below stay inside these ranges and needn't reach their ends.
Inputs may be any that keep to these rules, and one draw needn't show every extreme that they name: `bag_rows`: call the rows k * 512 to (k + 1) * 512 - 1 those of owner k. For each table, all slots of one device's 128 samples (used or not) name at most 32 distinct rows of any one owner, and every device names exactly 32 distinct rows of some owner in each table. Row indices may be held and sent in any lossless form.
All inputs are finite; a program needn't handle non-finite values. No bound on the sum of `labels` on one device may be relied on, other than what follows from the above.
Results may differ from the reference program's by a relative error of at most 0.0038.
The reference program's roundings to bfloat16 on the way count: a program that leaves them out, or rounds other values in their place, can miss the bound.
Values may be sent and summed in bfloat16 or wider, within the bound.
A program may use at most 128 MiB of HBM per device.

```python
import math
import jax
import jax.numpy as jnp
from jax import lax

E = 256
HID = 4096
NT = 2
MAXBAG = 16
CAP = 32
B_DEV = 128
ROWS_DEV = 512
D0 = 768
ROWS = 8192
BATCH = 4096
N_REPLICA = 2
N_SHARD = 16


def draw_bag_rows(key, part):
    groups = BATCH // B_DEV
    owners = ROWS // ROWS_DEV
    keys = jax.random.split(jax.random.fold_in(key, 7301), 6)
    perm_keys = jax.random.split(keys[0], groups * NT * owners)
    picks = jax.vmap(lambda one: jax.random.permutation(one, ROWS_DEV)[:CAP])(perm_keys).reshape(groups, NT, owners, CAP)
    order_keys = jax.random.split(keys[1], groups * NT)
    owner_order = jax.vmap(lambda one: jax.random.permutation(one, owners))(order_keys).reshape(groups, NT, owners)
    shape = (groups, B_DEV, NT, MAXBAG)
    owner_rank = jnp.minimum(jax.random.randint(keys[2], shape, 0, owners), jax.random.randint(keys[3], shape, 0, owners))
    choose = jnp.minimum(jax.random.randint(keys[4], shape, 0, CAP), jax.random.randint(keys[5], shape, 0, CAP))
    sample_ids = jnp.arange(B_DEV, dtype=jnp.int32)[None, :, None]
    forced = sample_ids < CAP
    owner_rank = owner_rank.at[:, :, :, 0].set(jnp.where(forced, 0, owner_rank[:, :, :, 0]))
    choose = choose.at[:, :, :, 0].set(jnp.where(forced, sample_ids % CAP, choose[:, :, :, 0]))
    group_ids = jnp.arange(groups, dtype=jnp.int32)[:, None, None, None]
    table_ids = jnp.arange(NT, dtype=jnp.int32)[None, None, :, None]
    owner = owner_order[group_ids, table_ids, owner_rank]
    local = picks[group_ids, table_ids, owner, choose]
    return (owner * ROWS_DEV + local).reshape(BATCH, NT, MAXBAG).astype(jnp.int32)


def with_ends(entries, own_key, least, top_value):
    index_at = [jax.random.randint(jax.random.fold_in(own_key, axis), (), 0, length) for axis, length in enumerate(entries.shape)]
    widest = entries.shape.index(max(entries.shape))
    neighbour = index_at[:widest] + [(index_at[widest] + 1) % entries.shape[widest]] + index_at[widest + 1:]
    return entries.at[tuple(index_at)].set(least).at[tuple(neighbour)].set(top_value)


def block_scale(own_key, shape, shards, least, top_value):
    level = 1.0
    for position, blocks in shards:
        steps = jax.random.uniform(jax.random.fold_in(jax.random.fold_in(own_key, 6), position), (blocks,), jnp.float32, least / len(shards), top_value / len(shards))
        level = level * jnp.repeat(jnp.exp(steps), shape[position] // blocks).reshape((-1,) + (1,) * (len(shape) - 1 - position))
    return level


def centred(key, dims, scale, most, shards=(), held_as=jnp.bfloat16):
    entries = scale * jax.random.normal(key, dims, jnp.float32)
    if shards:
        entries = entries * block_scale(key, dims, shards, -0.22, 0.18)
    return jnp.clip(entries, -most, most).astype(held_as)


def setup_inputs(seed: int = 0) -> dict:
    streams_of = jax.random.split(jax.random.key(seed), 12)
    return {
        "dense_input": centred(streams_of[0], (BATCH, E), 1.0, 6.0, ((0, 32),)),
        "bag_rows": draw_bag_rows(jax.random.fold_in(streams_of[11], 71), 0),
        "bag_lengths": with_ends(jax.random.randint(streams_of[2], (BATCH, NT), 1, MAXBAG + 1), jax.random.fold_in(streams_of[2], 1), 1, MAXBAG).astype(jnp.int32),
        "bag_weights": jnp.clip(jnp.exp(math.log(2.0) - 1.3862944 * jax.random.uniform(streams_of[3], (BATCH, NT, MAXBAG), jnp.float32) ** block_scale(streams_of[3], (BATCH, NT, MAXBAG), ((0, 32),), -0.2, 0.2)), 0.5, 2.0).astype(jnp.bfloat16),
        "labels": with_ends((jax.random.randint(streams_of[4], (BATCH,), 0, 4) < 1).astype(jnp.int32), jax.random.fold_in(streams_of[4], 1), 0, 1),
        "embedding": centred(streams_of[5], (ROWS, NT, E), 0.3, 2.0, ((0, 16),), jnp.float32),
        "first_moment": centred(streams_of[6], (ROWS, NT, E), 1.0, 6.0, ((0, 16),), jnp.float32),
        "second_moment": jnp.clip(jnp.exp(math.log(8.0) - 2.7725887 * jax.random.uniform(streams_of[7], (ROWS, NT), jnp.float32) ** block_scale(streams_of[7], (ROWS, NT), ((0, 16),), -0.2, 0.2)), 0.5, 8.0),
        "cross_weight": centred(streams_of[8], (D0, D0), D0 ** -0.5, 0.21875),
        "hidden_weight": centred(streams_of[9], (D0, HID), D0 ** -0.5, 0.21875),
        "head_weight": centred(streams_of[10], (HID,), HID ** -0.5, 0.09375),
    }


loss_scale = 64.0
beta_first = 0.9
beta_second = 0.99
epsilon = 1e-08

def dense_pass(dense_part, pooled, marks, cross_weight, hidden_weight, head_weight):
    samples = dense_part.shape[0]
    joined = jnp.concatenate([dense_part.astype(jnp.float32), pooled.reshape(samples, -1)], axis=1).astype(jnp.bfloat16)
    widened = joined.astype(jnp.float32)
    crossed = jnp.dot(joined, cross_weight, preferred_element_type=jnp.float32)
    layered = (widened * crossed + widened).astype(jnp.bfloat16)
    before = jnp.dot(layered, hidden_weight, preferred_element_type=jnp.float32)
    hidden = jnp.maximum(before, 0.0).astype(jnp.bfloat16)
    logits = jnp.dot(hidden, head_weight, preferred_element_type=jnp.float32)
    slope = (jax.nn.sigmoid(logits) - marks.astype(jnp.float32)) * loss_scale
    back_hidden = jnp.where(before > 0.0, slope[:, None] * head_weight.astype(jnp.float32)[None, :], 0.0).astype(jnp.bfloat16)
    back_layered = lax.dot_general(back_hidden, hidden_weight, (((1,), (1,)), ((), ())), preferred_element_type=jnp.float32)
    mixed = (back_layered * widened).astype(jnp.bfloat16)
    back_joined = back_layered * (crossed + 1.0) + lax.dot_general(mixed, cross_weight, (((1,), (1,)), ((), ())), preferred_element_type=jnp.float32)
    return back_joined[:, dense_part.shape[1]:].reshape(pooled.shape).astype(jnp.bfloat16)

def adam_rows(row_grad, hits, first_moment, second_moment):
    touched = hits > 0.0
    first_new = jnp.where(touched[:, :, None], beta_first * first_moment + (1.0 - beta_first) * row_grad, first_moment)
    second_new = jnp.where(touched, beta_second * second_moment + (1.0 - beta_second) * lax.optimization_barrier(jnp.mean(row_grad * row_grad, axis=2)), second_moment)
    step = jnp.where(touched[:, :, None], first_new / (jnp.sqrt(second_new)[:, :, None] + epsilon), 0.0)
    return (first_new, second_new, step)

def first_coefficients(bags, masses, usable):
    slots = bags.shape[2]
    slot_ids = jnp.arange(slots, dtype=jnp.int32)
    same = bags[:, :, :, None] == bags[:, :, None, :]
    summed = lax.optimization_barrier(jnp.sum(jnp.where(same, masses[:, :, None, :], 0.0), axis=3))
    earlier = same & usable[:, :, None, :] & (slot_ids[None, :] < slot_ids[:, None])[None, None, :, :]
    first = usable & jnp.logical_not(jnp.any(earlier, axis=3))
    rounded = lax.optimization_barrier(summed.astype(jnp.bfloat16))
    return jnp.where(first, rounded.astype(jnp.float32), 0.0)

def reference(dense_input, bag_rows, bag_lengths, bag_weights, labels, embedding, first_moment, second_moment, cross_weight, hidden_weight, head_weight):
    embedding_low = embedding.astype(jnp.bfloat16)
    group = B_DEV * N_SHARD
    tables = embedding.shape[1]
    width = embedding.shape[2]
    total_rows = embedding.shape[0]
    blocks = (dense_input.reshape(N_REPLICA, group, width), bag_rows.reshape(N_REPLICA, group, tables, -1), bag_lengths.reshape(N_REPLICA, group, tables), bag_weights.reshape(N_REPLICA, group, tables, -1), labels.reshape(N_REPLICA, group))

    def one_replica(carry, block):
        dense_part, bags, lengths, weights, marks = block
        slot_ids = jnp.arange(bags.shape[2], dtype=jnp.int32)
        usable = slot_ids[None, None, :] < lengths[:, :, None]
        masses = jnp.where(usable, weights.astype(jnp.float32), 0.0)
        slot_coef = first_coefficients(bags, masses, usable)
        pooled_list = []
        for which in range(tables):
            fetched = jnp.take(embedding_low[:, which, :], bags[:, which, :], axis=0).astype(jnp.float32)
            pooled_list.append(lax.optimization_barrier(jnp.sum(slot_coef[:, which, :, None] * fetched, axis=1)))
        pooled = jnp.stack(pooled_list, axis=1)
        bag_grads = dense_pass(dense_part, pooled, marks, cross_weight, hidden_weight, head_weight)
        grad_list = []
        count_list = []
        for which in range(tables):
            spread = slot_coef[:, which, :, None] * bag_grads[:, which, None, :].astype(jnp.float32)
            flat_ids = bags[:, which, :].reshape(-1)
            grad_list.append(jax.ops.segment_sum(spread.reshape(-1, width), flat_ids, num_segments=total_rows))
            count_list.append(jax.ops.segment_sum(usable[:, which, :].reshape(-1).astype(jnp.float32), flat_ids, num_segments=total_rows))
        row_grad = jnp.stack(grad_list, axis=1)
        hits = jnp.stack(count_list, axis=1)
        first_new, second_new, step = adam_rows(row_grad, hits, first_moment, second_moment)
        return ((carry[0] + first_new, carry[1] + second_new, carry[2] + step), None)
    start = (jnp.zeros(first_moment.shape, jnp.float32), jnp.zeros(second_moment.shape, jnp.float32), jnp.zeros(first_moment.shape, jnp.float32))
    sums, _ = lax.scan(one_replica, start, blocks)
    return (sums[0] / N_REPLICA, sums[1] / N_REPLICA, sums[2] / N_REPLICA)
```

```python
import functools

import jax
import jax.numpy as jnp
from jax import lax
from jax.experimental import pallas as pl
from jax.experimental.pallas import tpu as pltpu
from jax.sharding import PartitionSpec as P

loss_scale = 64.0
beta_first = 0.9
beta_second = 0.99
epsilon = 1e-08
CAP = 32
F32 = jnp.float32
BF16 = jnp.bfloat16
MESH = pl.DeviceIdType.MESH


def dot(a, b, ca, cb):
    return lax.dot_general(a, b, (((ca,), (cb,)), ((), ())), preferred_element_type=F32)


def vmem(count):
    return [pl.BlockSpec(memory_space=pltpu.VMEM)] * count


def column(row, eye):
    size = eye.shape[0]
    return jnp.concatenate(
        [
            jnp.sum(jnp.where(eye, row[:, lo : lo + size], 0.0), axis=1, keepdims=True)
            for lo in range(0, row.shape[1], size)
        ],
        axis=0,
    )


def flat(col, eye):
    size = eye.shape[0]
    return jnp.concatenate(
        [
            jnp.sum(jnp.where(eye, col[lo : lo + size], 0.0), axis=0, keepdims=True)
            for lo in range(0, col.shape[0], size)
        ],
        axis=1,
    )


def diagonal(size):
    a = lax.broadcasted_iota(jnp.int32, (size, size), 0)
    return a == lax.broadcasted_iota(jnp.int32, (size, size), 1)


def rank_rows(n, own_rows, ids, lengths, upper, loc_ref):
    slots, samples = ids.shape
    shift = own_rows.bit_length() - 1
    own_iota = lax.broadcasted_iota(jnp.int32, (n, samples), 0)
    loc_iota = lax.broadcasted_iota(jnp.int32, (own_rows, samples), 0)
    usable = lax.broadcasted_iota(jnp.int32, (slots, samples), 0) < lengths
    own = lax.shift_right_logical(ids, shift)
    loc = ids & (own_rows - 1)
    own_used = jnp.where(usable, own, -1)
    masks = [own_iota == own_used[s : s + 1] for s in range(slots)]
    all_own = jnp.concatenate([jnp.where(m, 1.0, 0.0).astype(BF16) for m in masks], axis=1)
    all_loc = jnp.concatenate(
        [jnp.where(loc_iota == loc[s : s + 1], 1.0, 0.0).astype(BF16) for s in range(slots)],
        axis=1,
    )
    seen = dot(all_own, all_loc, 1, 1) > 0.0
    rank = dot(jnp.where(seen, 1.0, 0.0).astype(BF16), upper, 1, 0)
    loc_ref[...] = all_loc
    return jnp.where(seen, rank, -1.0)


def coefficients(n, own_rows, ids, lengths, weights, q, loc_ref, ct_ref):
    slots, samples = ids.shape
    shift = own_rows.bit_length() - 1
    own_iota = lax.broadcasted_iota(jnp.int32, (n, samples), 0)
    usable = lax.broadcasted_iota(jnp.int32, (slots, samples), 0) < lengths
    own = lax.shift_right_logical(ids, shift)
    mass = jnp.where(usable, weights.astype(F32), 0.0)
    here = dot(q.astype(BF16), loc_ref[...], 1, 0)
    places = []
    for s in range(slots):
        mine = jnp.where(own_iota == own[s : s + 1], here[:, s * samples : (s + 1) * samples], 0.0)
        place = jnp.sum(mine, axis=0, keepdims=True)
        places.append(own[s : s + 1] * CAP + place.astype(jnp.int32))
    step = 128
    for base in range(0, n * CAP, step):
        pos_iota = lax.broadcasted_iota(jnp.int32, (step, samples), 0) + base
        total = jnp.zeros((step, samples), F32)
        for s in range(slots):
            total = total + jnp.where(pos_iota == places[s], mass[s : s + 1], 0.0)
        ct_ref[base : base + step, :] = total.astype(BF16)


def selector(rows):
    want = lax.broadcasted_iota(jnp.int32, (CAP, rows[0].shape[1]), 0).astype(F32)
    return jnp.concatenate(
        [jnp.where(want == row, 1.0, 0.0).astype(BF16) for row in rows], axis=0
    )


def place_rows(q_ref, sel_ref, hit_ref):
    n, _, own_rows = q_ref.shape
    q = jnp.concatenate([q_ref[s] for s in range(n)], axis=0).astype(BF16)
    source = lax.broadcasted_iota(jnp.int32, (n, n * CAP), 1) // CAP
    spread = jnp.where(lax.broadcasted_iota(jnp.int32, (n, n * CAP), 0) == source, 1.0, 0.0)
    ranks = dot(q, spread.astype(BF16), 0, 0)
    want = (lax.broadcasted_iota(jnp.int32, ranks.shape, 1) & (CAP - 1)).astype(F32)
    sel_ref[...] = jnp.where(ranks == want, 1.0, 0.0).astype(BF16)
    hit_ref[...] = jnp.max(ranks, axis=1, keepdims=True)


def adam_rows(reps, t, acc, hit, mom, v_ref, nm_ref, nv_ref, st_ref):
    own_rows = v_ref.shape[1]
    step = 128
    eye = diagonal(step)
    for lo in range(0, own_rows, step):
        at = slice(lo, lo + step)
        m = mom[at, t, :]
        v = column(v_ref[t : t + 1, at], eye)
        first = second = move = None
        for r in range(reps):
            grad = acc[r, at, :]
            touched = hit[t, r, at, :] >= 0.0
            new_m = jnp.where(touched, beta_first * m + (1.0 - beta_first) * grad, m)
            mean = jnp.mean(grad * grad, axis=1, keepdims=True)
            new_v = jnp.where(touched, beta_second * v + (1.0 - beta_second) * mean, v)
            scale = jnp.where(touched, 1.0 / (jnp.sqrt(new_v) + epsilon), 0.0)
            new_s = new_m * scale
            first = new_m if r == 0 else first + new_m
            second = new_v if r == 0 else second + new_v
            move = new_s if r == 0 else move + new_s
        nm_ref[at, t, :] = first * (1.0 / reps)
        nv_ref[t : t + 1, at] = flat(second, eye) * (1.0 / reps)
        st_ref[at, t, :] = move * (1.0 / reps)


def update_kernel(
    n, reps,
    rows_ref, len_ref, w_ref, dense_ref, mark_ref, head_ref, v_ref,
    emb_hbm, cross_hbm, hidden_hbm, m_hbm,
    nm_ref, nv_ref, st_ref,
    emb, cross, hid, mom, q_out, qi_ref, qo_ref, f_out, f_in, ct, before, g_out, ga_ref, locs,
    sel, hit, acc,
    load_sem, qs, qr, rs, rr, gs, gr, xs, xr, fs, fr,
):
    me = lax.axis_index("shard")
    rep = lax.axis_index("replica")
    tables, slots, samples = rows_ref.shape
    own_rows, _, width = emb.shape
    barrier = pltpu.get_barrier_semaphore()

    def hail(d, carry):
        pl.semaphore_signal(
            barrier, inc=1, device_id=(rep, lax.rem(me + d, n)), device_id_type=MESH
        )
        return carry

    lax.fori_loop(1, n, hail, 0)
    for r in range(1, reps):
        pl.semaphore_signal(
            barrier, inc=1, device_id=(lax.rem(rep + r, reps), me), device_id_type=MESH
        )
    load_emb = pltpu.make_async_copy(emb_hbm, emb, load_sem.at[0])
    load_cross = pltpu.make_async_copy(cross_hbm, cross, load_sem.at[1])
    load_hid = pltpu.make_async_copy(hidden_hbm, hid, load_sem.at[2])
    load_emb.start()
    load_cross.start()
    load_hid.start()
    load_mom = pltpu.make_async_copy(m_hbm, mom, load_sem.at[3])
    load_mom.start()

    def exchange(src, dst, send, recv, t, d):
        to = lax.rem(me + d, n)
        return pltpu.make_async_remote_copy(
            src_ref=src.at[t, to],
            dst_ref=dst.at[t, me],
            send_sem=send.at[t, d],
            recv_sem=recv.at[t, d],
            device_id=(rep, to),
            device_id_type=MESH,
        )

    def each(body):
        def run(d, carry):
            body(d)
            return carry

        lax.fori_loop(1, n, run, 0)

    def keep(src, dst, t):
        dst[t, me] = src[t, me]

    q_send = functools.partial(exchange, q_out, qi_ref, qs, qr)
    f_send = functools.partial(exchange, f_out, f_in, rs, rr)
    g_send = functools.partial(exchange, g_out, ga_ref.at[0], gs, gr)

    r0 = lax.broadcasted_iota(jnp.int32, (own_rows, own_rows), 0)
    r1 = lax.broadcasted_iota(jnp.int32, (own_rows, own_rows), 1)
    upper = jnp.where(r0 < r1, 1.0, 0.0).astype(BF16)
    ranks = []
    for t in range(tables):
        q = rank_rows(n, own_rows, rows_ref[t], len_ref[t], upper, locs.at[t])
        q_out[t, :, 0, :] = q
        ranks.append(q)
        if t == 0:
            pl.semaphore_wait(barrier, n - 1 + reps - 1)
        each(lambda d: q_send(t, d).start())
        keep(q_out, qi_ref, t)

    load_emb.wait()
    for t in range(tables):
        low = emb[:, t, :].astype(BF16)
        each(lambda d: q_send(t, d).wait_recv())
        got = dot(selector([qi_ref[t, s] for s in range(n)]), low, 1, 0).astype(BF16)
        f_out[t] = got.reshape(n, CAP, width)
        each(lambda d: f_send(t, d).start())
        keep(f_out, f_in, t)

    def q_pass(r):
        return pltpu.make_async_remote_copy(
            src_ref=qi_ref,
            dst_ref=qo_ref.at[r - 1],
            send_sem=xs.at[r - 1],
            recv_sem=xr.at[r - 1],
            device_id=(lax.rem(rep + r, reps), me),
            device_id_type=MESH,
        )

    for r in range(1, reps):
        q_pass(r).start()

    for t in range(tables):
        place_rows(qi_ref.at[t], sel.at[t, 0], hit.at[t, 0])
    for t in range(tables):
        coefficients(
            n, own_rows, rows_ref[t], len_ref[t], w_ref[t], ranks[t], locs.at[t], ct.at[t]
        )
    for r in range(1, reps):
        q_pass(r).wait_recv()
        for t in range(tables):
            place_rows(qo_ref.at[r - 1, t], sel.at[t, r], hit.at[t, r])
    marks = column(mark_ref[...].astype(F32), diagonal(samples))
    heads = head_ref[...].astype(F32)
    lanes = heads.shape[1]

    def head_chunk(base, count):
        first = base // lanes
        return jnp.concatenate(
            [heads[first + i : first + i + 1] for i in range(count // lanes)], axis=1
        )

    part = dense_ref.shape[1]
    pieces = [dense_ref[...]]
    load_cross.wait()
    crossed = dot(pieces[0], cross[:part, :], 1, 0)
    for t in range(tables):
        each(lambda d: f_send(t, d).wait_recv())
        pieces.append(dot(ct[t], f_in[t].reshape(n * CAP, width), 0, 0).astype(BF16))
        lo = part + t * width
        crossed = crossed + dot(pieces[-1], cross[lo : lo + width, :], 1, 0)
    joined = jnp.concatenate(pieces, axis=1)
    widened = joined.astype(F32)
    layered = (widened * crossed + widened).astype(BF16)
    load_hid.wait()
    units = hid.shape[1]
    chunk = 512
    logits = jnp.zeros((samples, 1), F32)
    for base in range(0, units, chunk):
        now = dot(layered, hid[:, base : base + chunk], 1, 0)
        before[:, base : base + chunk] = now
        hidden = jnp.maximum(now, 0.0).astype(BF16).astype(F32)
        head = head_chunk(base, chunk)
        logits = logits + jnp.sum(hidden * head, axis=1, keepdims=True)
    slope = (1.0 / (1.0 + jnp.exp(-logits)) - marks) * loss_scale
    back = jnp.zeros((samples, joined.shape[1]), F32)
    for base in range(0, units, chunk):
        head = head_chunk(base, chunk)
        push = jnp.where(before[:, base : base + chunk] > 0.0, slope * head, 0.0).astype(BF16)
        back = back + dot(push, hid[:, base : base + chunk], 1, 1)
    mixed = (back * widened).astype(BF16)
    for t in range(tables):
        lo = part + t * width
        grads = back[:, lo : lo + width] * (crossed[:, lo : lo + width] + 1.0) + dot(
            mixed, cross[lo : lo + width, :], 1, 1
        )
        sums = dot(ct[t], grads.astype(BF16), 1, 0).astype(BF16)
        g_out[t] = sums.reshape(n, CAP, width)
        each(lambda d: g_send(t, d).start())
        keep(g_out, ga_ref.at[0], t)

    def pass_on(r, t, d):
        frm = lax.rem(me + n - d, n)
        return pltpu.make_async_remote_copy(
            src_ref=ga_ref.at[0, t, frm],
            dst_ref=ga_ref.at[r, t, frm],
            send_sem=fs.at[r - 1, t, d],
            recv_sem=fr.at[r - 1, t, d],
            device_id=(lax.rem(rep + r, reps), me),
            device_id_type=MESH,
        )

    load_mom.wait()
    for t in range(tables):
        for r in range(1, reps):
            pass_on(r, t, 0).start()

        def relay(d):
            g_send(t, d).wait_recv()
            for r in range(1, reps):
                pass_on(r, t, d).start()

        each(relay)
        acc[0] = dot(sel[t, 0], ga_ref[0, t].reshape(n * CAP, width), 1, 0)
        for r in range(1, reps):
            pass_on(r, t, 0).wait_recv()

            def landed(d):
                pass_on(r, t, d).wait_recv()

            each(landed)
            acc[r] = dot(sel[t, r], ga_ref[r, t].reshape(n * CAP, width), 1, 0)
        adam_rows(reps, t, acc, hit, mom, v_ref, nm_ref, nv_ref, st_ref)
    for r in range(1, reps):
        q_pass(r).wait_send()
    for t in range(tables):
        for r in range(1, reps):
            pass_on(r, t, 0).wait_send()

        def finish(d):
            q_send(t, d).wait_send()
            f_send(t, d).wait_send()
            g_send(t, d).wait_send()
            for r in range(1, reps):
                pass_on(r, t, d).wait_send()

        each(finish)


def update(n, reps, rows, lengths, weights, dense, marks, head, second, embedding, cross, hidden, first):
    tables, slots, samples = rows.shape
    own_rows, _, width = embedding.shape
    dma = pltpu.SemaphoreType.DMA
    blocks = (tables, n, CAP, width)
    pair = dma((tables, n))
    wide = dma((reps - 1, tables, n))
    return pl.pallas_call(
        functools.partial(update_kernel, n, reps),
        out_shape=(
            pltpu.VMEM(first.shape, F32),
            pltpu.VMEM(second.shape, F32),
            pltpu.VMEM(first.shape, F32),
        ),
        in_specs=vmem(7) + [pl.BlockSpec(memory_space=pl.ANY)] * 4,
        out_specs=tuple(vmem(3)),
        scratch_shapes=[
            pltpu.VMEM(embedding.shape, F32),
            pltpu.VMEM(cross.shape, BF16),
            pltpu.VMEM(hidden.shape, BF16),
            pltpu.VMEM(first.shape, F32),
            pltpu.VMEM((tables, n, 1, own_rows), F32),
            pltpu.VMEM((tables, n, 1, own_rows), F32),
            pltpu.VMEM((reps - 1, tables, n, 1, own_rows), F32),
            pltpu.VMEM(blocks, BF16),
            pltpu.VMEM(blocks, BF16),
            pltpu.VMEM((tables, n * CAP, samples), BF16),
            pltpu.VMEM((samples, hidden.shape[1]), F32),
            pltpu.VMEM(blocks, BF16),
            pltpu.VMEM((reps,) + blocks, BF16),
            pltpu.VMEM((tables, own_rows, slots * samples), BF16),
            pltpu.VMEM((tables, reps, own_rows, n * CAP), BF16),
            pltpu.VMEM((tables, reps, own_rows, 1), F32),
            pltpu.VMEM((reps, own_rows, width), F32),
            dma((4,)),
            pair, pair, pair, pair, pair, pair,
            dma((reps - 1,)), dma((reps - 1,)),
            wide, wide,
        ],
        compiler_params=pltpu.CompilerParams(collective_id=0, has_side_effects=True),
        name="update",
    )(rows, lengths, weights, dense, marks, head, second, embedding, cross, hidden, first)


def emit_kernel(*refs):
    count = (len(refs) - 1) // 2
    sem = refs[-1]
    copies = [
        pltpu.make_async_copy(refs[i], refs[count + i], sem.at[i]) for i in range(count)
    ]
    for copy in copies:
        copy.start()
    for copy in copies:
        copy.wait()


def emit(*arrays):
    count = len(arrays)
    return pl.pallas_call(
        emit_kernel,
        out_shape=tuple(jax.ShapeDtypeStruct(a.shape, a.dtype) for a in arrays),
        in_specs=vmem(count),
        out_specs=tuple([pl.BlockSpec(memory_space=pl.ANY)] * count),
        scratch_shapes=[pltpu.SemaphoreType.DMA((count,))],
        name="emit",
    )(*[pltpu.with_memory_space_constraint(a, pltpu.VMEM) for a in arrays])


def local(
    reps,
    n,
    dense_input,
    bag_rows,
    bag_lengths,
    bag_weights,
    labels,
    embedding,
    first_moment,
    second_moment,
    cross_weight,
    hidden_weight,
    head_weight,
):
    first, second, step = emit(
        *update(
            n,
            reps,
            jnp.transpose(bag_rows, (1, 2, 0)),
            jnp.transpose(bag_lengths)[:, None, :],
            jnp.transpose(bag_weights, (1, 2, 0)),
            dense_input,
            labels[None, :],
            head_weight.reshape(-1, 128),
            jnp.transpose(second_moment),
            embedding,
            cross_weight,
            hidden_weight,
            first_moment,
        )
    )
    return first, jnp.transpose(second), step


def solution(mesh):
    placed = (
        P(("replica", "shard"), None),
        P(("replica", "shard"), None, None),
        P(("replica", "shard"), None),
        P(("replica", "shard"), None, None),
        P(("replica", "shard")),
        P("shard", None, None),
        P("shard", None, None),
        P("shard", None),
        P(),
        P(),
        P(),
    )
    return jax.shard_map(
        functools.partial(local, mesh.shape["replica"], mesh.shape["shard"]),
        mesh=mesh,
        in_specs=placed,
        out_specs=(P("shard", None, None), P("shard", None), P("shard", None, None)),
        check_vma=False,
    )
```

```python
import functools

import jax
import jax.numpy as jnp
from jax import lax
from jax.experimental import pallas as pl
from jax.experimental.pallas import tpu as pltpu
from jax.sharding import PartitionSpec as P

loss_scale = 64.0
beta_first = 0.9
beta_second = 0.99
epsilon = 1e-08
CAP = 32
F32 = jnp.float32
BF16 = jnp.bfloat16
MESH = pl.DeviceIdType.MESH


def dot(a, b, ca, cb):
    return lax.dot_general(a, b, (((ca,), (cb,)), ((), ())), preferred_element_type=F32)


def vmem(count):
    return [pl.BlockSpec(memory_space=pltpu.VMEM)] * count


LANES = 128


def lane_rows(x):
    rows, tables, width = x.shape
    x = x.reshape(rows, tables, width // LANES, LANES)
    return jnp.transpose(x, (0, 2, 1, 3)).reshape(-1, LANES)


def table_rows(x, rows, tables):
    x = jnp.transpose(x.reshape(rows, -1, tables, LANES), (0, 2, 1, 3))
    return x.reshape(rows, tables, -1)


def lane_slices(ref, tables, width, t, lo, count):
    tiles = width // LANES
    return [
        pl.ds(lo * tiles * tables + i * tables + t, count, stride=tiles * tables)
        for i in range(tiles)
    ]


def column(row, eye):
    size = eye.shape[0]
    return jnp.concatenate(
        [
            jnp.sum(jnp.where(eye, row[:, lo : lo + size], 0.0), axis=1, keepdims=True)
            for lo in range(0, row.shape[1], size)
        ],
        axis=0,
    )


def flat(col, eye):
    size = eye.shape[0]
    return jnp.concatenate(
        [
            jnp.sum(jnp.where(eye, col[lo : lo + size], 0.0), axis=0, keepdims=True)
            for lo in range(0, col.shape[0], size)
        ],
        axis=1,
    )


def diagonal(size):
    a = lax.broadcasted_iota(jnp.int32, (size, size), 0)
    return a == lax.broadcasted_iota(jnp.int32, (size, size), 1)


def rank_rows(n, own_rows, ids, lengths, upper, loc_ref):
    slots, samples = ids.shape
    shift = own_rows.bit_length() - 1
    own_iota = lax.broadcasted_iota(jnp.int32, (n, samples), 0)
    loc_iota = lax.broadcasted_iota(jnp.int32, (own_rows, samples), 0)
    usable = lax.broadcasted_iota(jnp.int32, (slots, samples), 0) < lengths
    own = lax.shift_right_logical(ids, shift)
    loc = ids & (own_rows - 1)
    own_used = jnp.where(usable, own, -1)
    masks = [own_iota == own_used[s : s + 1] for s in range(slots)]
    all_own = jnp.concatenate([jnp.where(m, 1.0, 0.0).astype(BF16) for m in masks], axis=1)
    all_loc = jnp.concatenate(
        [jnp.where(loc_iota == loc[s : s + 1], 1.0, 0.0).astype(BF16) for s in range(slots)],
        axis=1,
    )
    seen = dot(all_own, all_loc, 1, 1) > 0.0
    rank = dot(jnp.where(seen, 1.0, 0.0).astype(BF16), upper, 1, 0)
    loc_ref[...] = all_loc
    return jnp.where(seen, rank, -1.0)


def coefficients(n, own_rows, ids, lengths, weights, q, loc_ref, ct_ref):
    slots, samples = ids.shape
    shift = own_rows.bit_length() - 1
    own_iota = lax.broadcasted_iota(jnp.int32, (n, samples), 0)
    usable = lax.broadcasted_iota(jnp.int32, (slots, samples), 0) < lengths
    own = lax.shift_right_logical(ids, shift)
    mass = jnp.where(usable, weights.astype(F32), 0.0)
    here = dot(q.astype(BF16), loc_ref[...], 1, 0)
    places = []
    for s in range(slots):
        mine = jnp.where(own_iota == own[s : s + 1], here[:, s * samples : (s + 1) * samples], 0.0)
        place = jnp.sum(mine, axis=0, keepdims=True)
        places.append(own[s : s + 1] * CAP + place.astype(jnp.int32))
    step = 128
    for base in range(0, n * CAP, step):
        pos_iota = lax.broadcasted_iota(jnp.int32, (step, samples), 0) + base
        total = jnp.zeros((step, samples), F32)
        for s in range(slots):
            total = total + jnp.where(pos_iota == places[s], mass[s : s + 1], 0.0)
        ct_ref[base : base + step, :] = total.astype(BF16)


def selector(rows):
    want = lax.broadcasted_iota(jnp.int32, (CAP, rows[0].shape[1]), 0).astype(F32)
    return jnp.concatenate(
        [jnp.where(want == row, 1.0, 0.0).astype(BF16) for row in rows], axis=0
    )


def place_rows(q_ref, sel_ref, hit_ref):
    n, _, own_rows = q_ref.shape
    q = jnp.concatenate([q_ref[s] for s in range(n)], axis=0).astype(BF16)
    source = lax.broadcasted_iota(jnp.int32, (n, n * CAP), 1) // CAP
    spread = jnp.where(lax.broadcasted_iota(jnp.int32, (n, n * CAP), 0) == source, 1.0, 0.0)
    ranks = dot(q, spread.astype(BF16), 0, 0)
    want = (lax.broadcasted_iota(jnp.int32, ranks.shape, 1) & (CAP - 1)).astype(F32)
    sel_ref[...] = jnp.where(ranks == want, 1.0, 0.0).astype(BF16)
    hit_ref[...] = jnp.max(ranks, axis=1, keepdims=True)


def adam_rows(reps, t, acc, hit, mom, v_ref, vcol, nm_ref, nv_ref, st_ref):
    tables, own_rows = v_ref.shape
    width = acc.shape[2]
    step = 128
    eye = diagonal(step)
    for lo in range(0, own_rows, step):
        at = slice(lo, lo + step)
        spots = lane_slices(mom, tables, width, t, lo, step)
        m = jnp.concatenate([mom[spot, :] for spot in spots], axis=1)
        v = vcol[t, at, :]
        first = second = move = None
        for r in range(reps):
            grad = acc[r, at, :]
            touched = hit[t, r, at, :] >= 0.0
            new_m = jnp.where(touched, beta_first * m + (1.0 - beta_first) * grad, m)
            mean = jnp.mean(grad * grad, axis=1, keepdims=True)
            new_v = jnp.where(touched, beta_second * v + (1.0 - beta_second) * mean, v)
            scale = jnp.where(touched, 1.0 / (jnp.sqrt(new_v) + epsilon), 0.0)
            new_s = new_m * scale
            first = new_m if r == 0 else first + new_m
            second = new_v if r == 0 else second + new_v
            move = new_s if r == 0 else move + new_s
        first = first * (1.0 / reps)
        move = move * (1.0 / reps)
        for i, spot in enumerate(spots):
            lanes = slice(i * LANES, (i + 1) * LANES)
            nm_ref[spot, :] = first[:, lanes]
            st_ref[spot, :] = move[:, lanes]
        nv_ref[t : t + 1, at] = flat(second, eye) * (1.0 / reps)


def update_kernel(
    n, reps,
    rows_ref, len_ref, w_ref, dense_ref, mark_ref, head_ref, v_ref,
    emb_hbm, cross_hbm, hidden_hbm, m_hbm,
    nm_ref, nv_ref, st_ref,
    emb, cross, hid, mom, q_out, qi_ref, qo_ref, f_out, f_in, ct, before, g_out, ga_ref, locs,
    sel, hit, acc, vcol, lows,
    load_sem, qs, qr, rs, rr, gs, gr, xs, xr, fs, fr,
):
    me = lax.axis_index("shard")
    rep = lax.axis_index("replica")
    tables, slots, samples = rows_ref.shape
    own_rows, width = q_out.shape[3], f_out.shape[3]
    barrier = pltpu.get_barrier_semaphore()

    def hail(d, carry):
        pl.semaphore_signal(
            barrier, inc=1, device_id=(rep, lax.rem(me + d, n)), device_id_type=MESH
        )
        return carry

    lax.fori_loop(1, n, hail, 0)
    for r in range(1, reps):
        pl.semaphore_signal(
            barrier, inc=1, device_id=(lax.rem(rep + r, reps), me), device_id_type=MESH
        )
    load_emb = pltpu.make_async_copy(emb_hbm, emb, load_sem.at[0])
    load_cross = pltpu.make_async_copy(cross_hbm, cross, load_sem.at[1])
    load_hid = pltpu.make_async_copy(hidden_hbm, hid, load_sem.at[2])
    load_emb.start()
    load_cross.start()
    load_hid.start()
    load_mom = pltpu.make_async_copy(m_hbm, mom, load_sem.at[3])
    load_mom.start()

    def exchange(src, dst, send, recv, t, d):
        to = lax.rem(me + d, n)
        return pltpu.make_async_remote_copy(
            src_ref=src.at[t, to],
            dst_ref=dst.at[t, me],
            send_sem=send.at[t, d],
            recv_sem=recv.at[t, d],
            device_id=(rep, to),
            device_id_type=MESH,
        )

    def each(body):
        def run(d, carry):
            body(d)
            return carry

        lax.fori_loop(1, n, run, 0)

    def keep(src, dst, t):
        dst[t, me] = src[t, me]

    q_send = functools.partial(exchange, q_out, qi_ref, qs, qr)
    f_send = functools.partial(exchange, f_out, f_in, rs, rr)
    g_send = functools.partial(exchange, g_out, ga_ref.at[0], gs, gr)

    r0 = lax.broadcasted_iota(jnp.int32, (own_rows, own_rows), 0)
    r1 = lax.broadcasted_iota(jnp.int32, (own_rows, own_rows), 1)
    upper = jnp.where(r0 < r1, 1.0, 0.0).astype(BF16)
    ranks = []
    for t in range(tables):
        q = rank_rows(n, own_rows, rows_ref[t], len_ref[t], upper, locs.at[t])
        q_out[t, :, 0, :] = q
        ranks.append(q)
        if t == 0:
            pl.semaphore_wait(barrier, n - 1 + reps - 1)
        each(lambda d: q_send(t, d).start())
        keep(q_out, qi_ref, t)

    load_emb.wait()
    for t in range(tables):
        lows[t] = jnp.concatenate(
            [emb[spot, :] for spot in lane_slices(emb, tables, width, t, 0, own_rows)], axis=1
        ).astype(BF16)
    group = 1 << (n.bit_length() // 2)
    for base in range(n - group, -1, -group):
        for t in range(tables):
            for s in range(base, base + group):

                @pl.when(me != s)
                def _():
                    q_send(t, lax.rem(me + n - s, n)).wait_recv()

            picks = selector([qi_ref[t, s] for s in range(base, base + group)])
            got = dot(picks, lows[t], 1, 0).astype(BF16)
            f_out[t, base : base + group] = got.reshape(group, CAP, width)
            for s in range(base, base + group):

                @pl.when(me != s)
                def _():
                    f_send(t, lax.rem(s + n - me, n)).start()

    for t in range(tables):
        keep(f_out, f_in, t)

    def q_pass(r):
        return pltpu.make_async_remote_copy(
            src_ref=qi_ref,
            dst_ref=qo_ref.at[r - 1],
            send_sem=xs.at[r - 1],
            recv_sem=xr.at[r - 1],
            device_id=(lax.rem(rep + r, reps), me),
            device_id_type=MESH,
        )

    for r in range(1, reps):
        q_pass(r).start()

    for t in range(tables):
        place_rows(qi_ref.at[t], sel.at[t, 0], hit.at[t, 0])
        vcol[t] = column(v_ref[t : t + 1, :], diagonal(LANES))
    for t in range(tables):
        coefficients(
            n, own_rows, rows_ref[t], len_ref[t], w_ref[t], ranks[t], locs.at[t], ct.at[t]
        )
    for r in range(1, reps):
        q_pass(r).wait_recv()
        for t in range(tables):
            place_rows(qo_ref.at[r - 1, t], sel.at[t, r], hit.at[t, r])
    marks = column(mark_ref[...].astype(F32), diagonal(samples))
    heads = head_ref[...].astype(F32)
    lanes = heads.shape[1]

    def head_chunk(base, count):
        first = base // lanes
        return jnp.concatenate(
            [heads[first + i : first + i + 1] for i in range(count // lanes)], axis=1
        )

    part = dense_ref.shape[1]
    pieces = [dense_ref[...]]
    load_cross.wait()
    crossed = dot(pieces[0], cross[:part, :], 1, 0)
    for t in range(tables):
        each(lambda d: f_send(t, d).wait_recv())
        pieces.append(dot(ct[t], f_in[t].reshape(n * CAP, width), 0, 0).astype(BF16))
        lo = part + t * width
        crossed = crossed + dot(pieces[-1], cross[lo : lo + width, :], 1, 0)
    joined = jnp.concatenate(pieces, axis=1)
    widened = joined.astype(F32)
    layered = (widened * crossed + widened).astype(BF16)
    load_hid.wait()
    units = hid.shape[1]
    chunk = 512
    logits = jnp.zeros((samples, 1), F32)
    for base in range(0, units, chunk):
        now = dot(layered, hid[:, base : base + chunk], 1, 0)
        before[:, base : base + chunk] = now
        hidden = jnp.maximum(now, 0.0).astype(BF16).astype(F32)
        head = head_chunk(base, chunk)
        logits = logits + jnp.sum(hidden * head, axis=1, keepdims=True)
    slope = (1.0 / (1.0 + jnp.exp(-logits)) - marks) * loss_scale
    back = jnp.zeros((samples, joined.shape[1]), F32)
    for base in range(0, units, chunk):
        head = head_chunk(base, chunk)
        push = jnp.where(before[:, base : base + chunk] > 0.0, slope * head, 0.0).astype(BF16)
        back = back + dot(push, hid[:, base : base + chunk], 1, 1)
    mixed = (back * widened).astype(BF16)
    for t in range(tables):
        lo = part + t * width
        grads = back[:, lo : lo + width] * (crossed[:, lo : lo + width] + 1.0) + dot(
            mixed, cross[lo : lo + width, :], 1, 1
        )
        sums = dot(ct[t], grads.astype(BF16), 1, 0).astype(BF16)
        g_out[t] = sums.reshape(n, CAP, width)
        each(lambda d: g_send(t, d).start())
        keep(g_out, ga_ref.at[0], t)

    def pass_on(r, t, d):
        frm = lax.rem(me + n - d, n)
        return pltpu.make_async_remote_copy(
            src_ref=ga_ref.at[0, t, frm],
            dst_ref=ga_ref.at[r, t, frm],
            send_sem=fs.at[r - 1, t, d],
            recv_sem=fr.at[r - 1, t, d],
            device_id=(lax.rem(rep + r, reps), me),
            device_id_type=MESH,
        )

    load_mom.wait()
    for t in range(tables):
        for r in range(1, reps):
            pass_on(r, t, 0).start()

        def relay(d):
            g_send(t, d).wait_recv()
            for r in range(1, reps):
                pass_on(r, t, d).start()

        each(relay)
        acc[0] = dot(sel[t, 0], ga_ref[0, t].reshape(n * CAP, width), 1, 0)
        for r in range(1, reps):
            pass_on(r, t, 0).wait_recv()

            def landed(d):
                pass_on(r, t, d).wait_recv()

            each(landed)
            acc[r] = dot(sel[t, r], ga_ref[r, t].reshape(n * CAP, width), 1, 0)
        adam_rows(reps, t, acc, hit, mom, v_ref, vcol, nm_ref, nv_ref, st_ref)
    for r in range(1, reps):
        q_pass(r).wait_send()
    for t in range(tables):
        for r in range(1, reps):
            pass_on(r, t, 0).wait_send()

        def finish(d):
            q_send(t, d).wait_send()
            f_send(t, d).wait_send()
            g_send(t, d).wait_send()
            for r in range(1, reps):
                pass_on(r, t, d).wait_send()

        each(finish)


def update(n, reps, rows, lengths, weights, dense, marks, head, second, embedding, cross, hidden, first):
    tables, slots, samples = rows.shape
    own_rows = second.shape[1]
    width = dense.shape[1]
    dma = pltpu.SemaphoreType.DMA
    blocks = (tables, n, CAP, width)
    pair = dma((tables, n))
    wide = dma((reps - 1, tables, n))
    return pl.pallas_call(
        functools.partial(update_kernel, n, reps),
        out_shape=(
            pltpu.VMEM(first.shape, F32),
            pltpu.VMEM(second.shape, F32),
            pltpu.VMEM(first.shape, F32),
        ),
        in_specs=vmem(7) + [pl.BlockSpec(memory_space=pl.ANY)] * 4,
        out_specs=tuple(vmem(3)),
        scratch_shapes=[
            pltpu.VMEM(embedding.shape, F32),
            pltpu.VMEM(cross.shape, BF16),
            pltpu.VMEM(hidden.shape, BF16),
            pltpu.VMEM(first.shape, F32),
            pltpu.VMEM((tables, n, 1, own_rows), F32),
            pltpu.VMEM((tables, n, 1, own_rows), F32),
            pltpu.VMEM((reps - 1, tables, n, 1, own_rows), F32),
            pltpu.VMEM(blocks, BF16),
            pltpu.VMEM(blocks, BF16),
            pltpu.VMEM((tables, n * CAP, samples), BF16),
            pltpu.VMEM((samples, hidden.shape[1]), F32),
            pltpu.VMEM(blocks, BF16),
            pltpu.VMEM((reps,) + blocks, BF16),
            pltpu.VMEM((tables, own_rows, slots * samples), BF16),
            pltpu.VMEM((tables, reps, own_rows, n * CAP), BF16),
            pltpu.VMEM((tables, reps, own_rows, 1), F32),
            pltpu.VMEM((reps, own_rows, width), F32),
            pltpu.VMEM((tables, own_rows, 1), F32),
            pltpu.VMEM((tables, own_rows, width), BF16),
            dma((4,)),
            pair, pair, pair, pair, pair, pair,
            dma((reps - 1,)), dma((reps - 1,)),
            wide, wide,
        ],
        compiler_params=pltpu.CompilerParams(collective_id=0, has_side_effects=True),
        name="update",
    )(rows, lengths, weights, dense, marks, head, second, embedding, cross, hidden, first)


def emit_kernel(*refs):
    count = (len(refs) - 1) // 2
    sem = refs[-1]
    copies = [
        pltpu.make_async_copy(refs[i], refs[count + i], sem.at[i]) for i in range(count)
    ]
    for copy in copies:
        copy.start()
    for copy in copies:
        copy.wait()


def emit(*arrays):
    count = len(arrays)
    return pl.pallas_call(
        emit_kernel,
        out_shape=tuple(jax.ShapeDtypeStruct(a.shape, a.dtype) for a in arrays),
        in_specs=vmem(count),
        out_specs=tuple([pl.BlockSpec(memory_space=pl.ANY)] * count),
        scratch_shapes=[pltpu.SemaphoreType.DMA((count,))],
        name="emit",
    )(*[pltpu.with_memory_space_constraint(a, pltpu.VMEM) for a in arrays])


def local(
    reps,
    n,
    dense_input,
    bag_rows,
    bag_lengths,
    bag_weights,
    labels,
    embedding,
    first_moment,
    second_moment,
    cross_weight,
    hidden_weight,
    head_weight,
):
    first, second, step = emit(
        *update(
            n,
            reps,
            jnp.transpose(bag_rows, (1, 2, 0)),
            jnp.transpose(bag_lengths)[:, None, :],
            jnp.transpose(bag_weights, (1, 2, 0)),
            dense_input,
            labels[None, :],
            head_weight.reshape(-1, 128),
            jnp.transpose(second_moment),
            lane_rows(embedding),
            cross_weight,
            hidden_weight,
            lane_rows(first_moment),
        )
    )
    rows, tables, _ = embedding.shape
    return (
        table_rows(first, rows, tables),
        jnp.transpose(second),
        table_rows(step, rows, tables),
    )


def solution(mesh):
    placed = (
        P(("replica", "shard"), None),
        P(("replica", "shard"), None, None),
        P(("replica", "shard"), None),
        P(("replica", "shard"), None, None),
        P(("replica", "shard")),
        P("shard", None, None),
        P("shard", None, None),
        P("shard", None),
        P(),
        P(),
        P(),
    )
    return jax.shard_map(
        functools.partial(local, mesh.shape["replica"], mesh.shape["shard"]),
        mesh=mesh,
        in_specs=placed,
        out_specs=(P("shard", None, None), P("shard", None), P("shard", None, None)),
        check_vma=False,
    )
```
